512 devices in a mesh: req: 128 (over x, z, core), ctx: 4 (over y).
Axes of the slice: x: 4, y: 4, z: 16, core: 2. Of those that a mesh axis runs over, the one named last changes fastest.
Arguments:
- prefill_residual: bfloat16 [131072, 1536], P(('req', 'ctx')), may hold values from -1.75 to 1.75
- prompt_queries: bfloat16 [131072, 1536], P(('req', 'ctx')), may hold values from -100 to 100
- prompt_keys: bfloat16 [131072, 512], P(('req', 'ctx')), may hold values from -12 to 12
- prompt_values: bfloat16 [131072, 512], P(('req', 'ctx')), may hold values from -6 to 6
- out_weight: bfloat16 [1536, 1536], P(None, 'ctx'), may hold values from -0.15625 to 0.15625
- prompt_token_counts: int32 [128, 3], P('req'), may hold values from 1 to 512, 1024 in all within a row
- page_dest: int32 [128, 128, 1], P('req'), may hold values from 0 to 127; in each aligned block of 128 rows (0 to 127, 128 to 255, ..., all dimensions but the last counted through in order) at most 2 rows name the same one
- decode_residual: bfloat16 [128, 3, 1536], P('req', None, 'ctx'), may hold values from -1.75 to 1.75
- decoded_queries: bfloat16 [128, 3, 1536], P('req', None, 'ctx'), may hold values from -300 to 300
- decoded_keys: bfloat16 [128, 3, 512], P('req', None, 'ctx'), may hold values from -12 to 12
- decoded_values: bfloat16 [128, 3, 512], P('req', None, 'ctx'), may hold values from -6 to 6
Outputs:
- prefill_out: bfloat16 [131072, 1536], P(('req', 'ctx'))
- target_page_store: bfloat16 [128, 256, 8, 2, 512], P('req', None, None, None, 'ctx')
- decode_out: bfloat16 [128, 3, 1536], P('req', None, 'ctx')
The draws below stay inside these ranges and needn't reach their ends.
Inputs may be any that keep to these rules, and one draw needn't show every extreme that they name: `prompt_token_counts`: each row sums to 1024; the largest prompt of every group has exactly 512 tokens. `page_dest`: at most 2 pages of one group go to one destination group, and in every draw some group sends exactly 2 pages to one destination.
All inputs are finite; a program needn't handle non-finite values.
Results may differ from the reference program's by a relative error of at most 0.0075.
Values may be sent and summed in bfloat16 or wider, within the bound.
No kernel may reach another device: no remote copies, remote signals or barrier semaphores. Data moves between devices by JAX's collectives and lax.ppermute only.
A program may use at most 128 MiB of HBM per device.

```python
import math
import jax
import jax.numpy as jnp
import numpy as np
from jax import lax

MODEL_WIDTH = 1536
QUERY_HEADS = 24
KEY_VALUE_HEADS = 8
HEAD_SIZE = 64
GROUP_PROMPTS = 3
PAGE_TOKENS = 8
GROUP_TOKENS = 1024
PREFILL_TOKENS = 131072
MOSTL = 512
GROUP_PAGES = 128
CAP = 2
PAGE_SLOTS = 256
N_REQ = 128


def prefill_parts(key):
    key_row_block = jnp.clip(jax.random.normal(jax.random.fold_in(key, 7001), (PREFILL_TOKENS, KEY_VALUE_HEADS * HEAD_SIZE), jnp.float32), -5.0, 5.0)
    query_rows = jnp.clip(jax.random.normal(jax.random.fold_in(key, 7002), (PREFILL_TOKENS, QUERY_HEADS * HEAD_SIZE), jnp.float32), -5.0, 5.0)
    return (query_rows, key_row_block)


def decode_parts(key):
    fresh_query = jnp.clip(jax.random.normal(jax.random.fold_in(key, 7003), (N_REQ, GROUP_PROMPTS, QUERY_HEADS * HEAD_SIZE), jnp.float32), -5.0, 5.0)
    fresh_key = jnp.clip(jax.random.normal(jax.random.fold_in(key, 7004), (N_REQ, GROUP_PROMPTS, KEY_VALUE_HEADS * HEAD_SIZE), jnp.float32), -5.0, 5.0)
    return (fresh_query, fresh_key)


def draw_prompt_queries(key, part):
    return prefill_parts(key)[0].astype(jnp.bfloat16)


def draw_prompt_keys(key, part):
    return prefill_parts(key)[1].astype(jnp.bfloat16)


def draw_decoded_queries(key, part):
    return decode_parts(key)[0].astype(jnp.bfloat16)


def draw_decoded_keys(key, part):
    return decode_parts(key)[1].astype(jnp.bfloat16)


def steps_of(own_key, shape, pieces, smallest, largest):
    def one(position, blocks):
        draws = jax.random.uniform(jax.random.fold_in(jax.random.fold_in(own_key, 6), position), (blocks,), jnp.float32, smallest / len(pieces), largest / len(pieces))
        return jnp.repeat(jnp.exp(draws), shape[position] // blocks).reshape((-1,) + (1,) * (len(shape) - position - 1))

    gain = one(*pieces[0])
    for cut in pieces[1:]:
        gain = gain * one(*cut)
    return gain


def split_up(count, total, limit, slope):
    weights = [(1 << 20) // math.isqrt(grade ** slope) + 1 for grade in range(2, count + 1)]
    spare, holding = total - limit - (count - 1), [1] * (count - 1)
    while spare > 0:
        free = [i for i in range(count - 1) if holding[i] < limit]
        whole, remaining = sum([weights[i] for i in free]), spare
        for i in free:
            more = min(limit - holding[i], max(1, remaining * weights[i] // whole), spare)
            holding[i] = holding[i] + more
            spare = spare - more
    return np.array([limit] + holding)


def ragged(key, amount, total, bound, slope):
    if amount == 2:
        one = jax.random.randint(key, (), max(1, total - bound), min(bound, total - 1) + 1)
        return jnp.stack([one, total - one])
    lengths = jnp.asarray(split_up(amount, total, bound, slope), jnp.int32)
    pairs = (amount - 1) // 2
    giver, receiver = lengths[1:1 + 2 * pairs:2], lengths[2:2 + 2 * pairs:2]
    room = jnp.minimum(giver - 1, bound - receiver)
    moved = jax.random.randint(jax.random.fold_in(key, 1), (pairs,), 0, 1 << 20) % (room + 1)
    lengths = lengths.at[1:1 + 2 * pairs:2].set(giver - moved).at[2:2 + 2 * pairs:2].set(receiver + moved)
    return lengths[jax.random.permutation(jax.random.fold_in(key, 2), amount)]


def assign_block(own_key, own, number, rows, count, top, bound, lean):
    ranking = jax.random.permutation(own_key, count)
    heavy_load, ordinary = shares(count, rows * top, bound, lean, True), shares(count, rows * top, bound, lean, False)
    places = jnp.arange(count)

    def named(lengths, rotation):
        used = int((lengths > 0).sum())
        fixed = max(1, used // 4)
        passed = fixed + (places - fixed + rotation * (used - fixed)) % max(1, count - fixed)
        return jnp.zeros((count,), jnp.int32).at[ranking[jnp.where(places < fixed, places, passed)]].set(jnp.asarray(lengths, jnp.int32))

    lengths = jnp.where(number % 4 == 0, named(heavy_load, number // 4), named(ordinary, number - number // 4 - 1))
    mixed = jax.random.permutation(jax.random.fold_in(own, 3), count)
    giver, sink = mixed[0:count // 2 * 2:2], mixed[1:count // 2 * 2:2]
    slack = jnp.minimum(lengths[giver] - 1, bound - lengths[sink]) // 2
    slack = jnp.where((giver == ranking[0]) | (sink == ranking[0]) | (lengths[sink] == 0), 0, jnp.maximum(slack, 0))
    passed = jax.random.randint(jax.random.fold_in(own, 4), (count // 2,), 0, 1 << 20) % (slack + 1)
    lengths = lengths.at[giver].add(-passed).at[sink].add(passed)
    labels = jnp.searchsorted(jnp.cumsum(lengths), jnp.arange(rows * top), side="right").astype(jnp.int32)
    grid = labels.reshape(top, rows).T
    grid = grid[jax.random.permutation(jax.random.fold_in(own, 1), rows)]
    rotation = jax.random.randint(jax.random.fold_in(own, 2), (rows, 1), 0, top)
    return jnp.take_along_axis(grid, (jnp.arange(top)[None, :] + rotation) % top, axis=1)


def shares(amount, total, reach, lean, full):
    loads = [(1 << 20) // math.isqrt(rank ** lean) + 1 for rank in range(1, amount + 1)]
    largest = reach if full else min(reach, max(-(-total // amount), total * loads[0] // sum(loads)))
    least = 1 if total - largest >= amount - 1 else 0
    holding, spare = [largest] + [least] * (amount - 1), total - largest - least * (amount - 1)
    while spare > 0:
        candidates = [i for i in range(1, amount) if holding[i] < largest] or [i for i in range(1, amount) if holding[i] < reach]
        pool, left = sum([loads[i] for i in candidates]), spare
        for i in candidates:
            more = min(reach - holding[i], max(1, left * loads[i] // pool), spare)
            holding[i] = holding[i] + more
            spare = spare - more
    return np.array(holding)


def normal_values(stream_key, dims, deviation, most, pieces=(), kind=jnp.bfloat16):
    gain = steps_of(stream_key, dims, pieces, -0.22, 0.18) if pieces else 1.0
    drawn = jax.random.normal(stream_key, dims, jnp.float32) * deviation * gain
    return jnp.minimum(jnp.maximum(drawn, -most), most).astype(kind)


def setup_inputs(seed: int = 0) -> dict:
    seeds = jax.random.split(jax.random.key(seed), 12)
    prefill_residual = normal_values(seeds[0], (PREFILL_TOKENS, MODEL_WIDTH), 0.3, 1.75, ((0, 512),))
    prompt_queries = draw_prompt_queries(jax.random.fold_in(seeds[11], 71), 0)
    prompt_keys = draw_prompt_keys(jax.random.fold_in(seeds[11], 71), 0)
    prompt_values = normal_values(seeds[3], (PREFILL_TOKENS, KEY_VALUE_HEADS * HEAD_SIZE), 1.0, 6.0, ((0, 512),))
    out_weight = normal_values(seeds[4], (QUERY_HEADS * HEAD_SIZE, MODEL_WIDTH), (QUERY_HEADS * HEAD_SIZE) ** -0.5, 0.15625, ((1, 4),))
    prompt_token_counts = jax.vmap(lambda own: ragged(own, GROUP_PROMPTS, GROUP_TOKENS, MOSTL, 2))(jax.random.split(seeds[5], N_REQ)).reshape((N_REQ, GROUP_PROMPTS)).astype(jnp.int32)
    page_dest_keys = jax.random.split(jax.random.fold_in(seeds[6], 1), N_REQ * GROUP_PAGES // GROUP_PAGES)
    page_dest_turns = jax.random.permutation(jax.random.fold_in(seeds[6], 3), N_REQ * GROUP_PAGES // GROUP_PAGES)
    page_dest = jax.vmap(lambda own, number: assign_block(jax.random.fold_in(seeds[6], 2), own, number, GROUP_PAGES, N_REQ, 1, CAP, 2))(page_dest_keys, page_dest_turns).reshape((N_REQ, GROUP_PAGES, 1))
    decode_residual = normal_values(seeds[7], (N_REQ, GROUP_PROMPTS, MODEL_WIDTH), 0.3, 1.75, ((0, 128), (2, 4)))
    decoded_queries = draw_decoded_queries(jax.random.fold_in(seeds[11], 71), 0)
    decoded_keys = draw_decoded_keys(jax.random.fold_in(seeds[11], 71), 0)
    decoded_values = normal_values(seeds[10], (N_REQ, GROUP_PROMPTS, KEY_VALUE_HEADS * HEAD_SIZE), 1.0, 6.0, ((0, 128), (2, 4)))
    return dict(prefill_residual=prefill_residual, prompt_queries=prompt_queries, prompt_keys=prompt_keys, prompt_values=prompt_values, out_weight=out_weight, prompt_token_counts=prompt_token_counts, page_dest=page_dest, decode_residual=decode_residual, decoded_queries=decoded_queries, decoded_keys=decoded_keys, decoded_values=decoded_values)


masked_score = -1e+30

def prompt_ids(lengths_row, positions):
    prompt_ends = jnp.cumsum(lengths_row).astype(jnp.int32)
    return lax.optimization_barrier(jnp.sum((positions[:, None] >= prompt_ends[None, :]).astype(jnp.int32), axis=1)).astype(jnp.int32)

def one_group(group_arguments, out_weight):
    x_group, query_group, key_group, value_group, lengths_row, new_x, fresh_query, fresh_key, fresh_value = group_arguments
    queries_per_key_head = QUERY_HEADS // KEY_VALUE_HEADS
    logit_scale = 1.0 / math.sqrt(HEAD_SIZE)
    positions = jnp.arange(GROUP_TOKENS, dtype=jnp.int32)
    prompt_of = prompt_ids(lengths_row, positions)
    allowed = (prompt_of[:, None] == prompt_of[None, :]) & (positions[None, :] <= positions[:, None])
    query_grouped = query_group.astype(jnp.float32).reshape(GROUP_TOKENS, KEY_VALUE_HEADS, queries_per_key_head, HEAD_SIZE)
    key_heads = key_group.astype(jnp.float32).reshape(GROUP_TOKENS, KEY_VALUE_HEADS, HEAD_SIZE)
    value_heads = value_group.astype(jnp.float32).reshape(GROUP_TOKENS, KEY_VALUE_HEADS, HEAD_SIZE)
    scores = jnp.einsum('tgrd,mgd->tgrm', query_grouped, key_heads, precision=lax.Precision.HIGHEST) * logit_scale
    visible = allowed[:, None, None, :]
    scores = jnp.where(visible, scores, masked_score)
    row_max = lax.optimization_barrier(jnp.max(scores, axis=-1))
    weights = jnp.where(visible, jnp.exp(scores - row_max[..., None]), 0.0)
    total = lax.optimization_barrier(jnp.sum(weights, axis=-1))
    weighted = jnp.einsum('tgrm,mgd->tgrd', weights.astype(jnp.bfloat16).astype(jnp.float32), value_heads, precision=lax.Precision.HIGHEST)
    attention = (weighted / total[..., None]).reshape(GROUP_TOKENS, QUERY_HEADS * HEAD_SIZE).astype(jnp.bfloat16)
    prefill = (x_group.astype(jnp.float32) + jnp.dot(attention, out_weight, preferred_element_type=jnp.float32)).astype(jnp.bfloat16)
    fresh_query_grouped = fresh_query.astype(jnp.float32).reshape(GROUP_PROMPTS, KEY_VALUE_HEADS, queries_per_key_head, HEAD_SIZE)
    dec_scores = jnp.einsum('rgqd,mgd->rgqm', fresh_query_grouped, key_heads, precision=lax.Precision.HIGHEST) * logit_scale
    dec_allowed = prompt_of[None, :] == jnp.arange(GROUP_PROMPTS, dtype=jnp.int32)[:, None]
    dec_visible = dec_allowed[:, None, None, :]
    dec_scores = jnp.where(dec_visible, dec_scores, masked_score)
    self_score = lax.optimization_barrier(jnp.sum(fresh_query_grouped * fresh_key.astype(jnp.float32).reshape(GROUP_PROMPTS, KEY_VALUE_HEADS, 1, HEAD_SIZE), axis=-1)) * logit_scale
    dec_max = jnp.maximum(lax.optimization_barrier(jnp.max(dec_scores, axis=-1)), self_score)
    dec_weights = jnp.where(dec_visible, jnp.exp(dec_scores - dec_max[..., None]), 0.0)
    self_weight = jnp.exp(self_score - dec_max)
    dec_total = lax.optimization_barrier(jnp.sum(dec_weights, axis=-1)) + self_weight
    decode_weighted_sum = jnp.einsum('rgqm,mgd->rgqd', dec_weights.astype(jnp.bfloat16).astype(jnp.float32), value_heads, precision=lax.Precision.HIGHEST)
    decode_weighted_sum = decode_weighted_sum + self_weight.astype(jnp.bfloat16).astype(jnp.float32)[..., None] * fresh_value.astype(jnp.float32).reshape(GROUP_PROMPTS, KEY_VALUE_HEADS, 1, HEAD_SIZE)
    new_attention = (decode_weighted_sum / dec_total[..., None]).reshape(GROUP_PROMPTS, QUERY_HEADS * HEAD_SIZE).astype(jnp.bfloat16)
    decoded = (new_x.astype(jnp.float32) + jnp.dot(new_attention, out_weight, preferred_element_type=jnp.float32)).astype(jnp.bfloat16)
    return (prefill, decoded)

def reference(prefill_residual, prompt_queries, prompt_keys, prompt_values, out_weight, prompt_token_counts, page_dest, decode_residual, decoded_queries, decoded_keys, decoded_values):
    group_arguments = (prefill_residual.reshape(N_REQ, GROUP_TOKENS, MODEL_WIDTH), prompt_queries.reshape(N_REQ, GROUP_TOKENS, QUERY_HEADS * HEAD_SIZE), prompt_keys.reshape(N_REQ, GROUP_TOKENS, KEY_VALUE_HEADS * HEAD_SIZE), prompt_values.reshape(N_REQ, GROUP_TOKENS, KEY_VALUE_HEADS * HEAD_SIZE), prompt_token_counts, decode_residual, decoded_queries, decoded_keys, decoded_values)
    prefill, decoded = lax.map(lambda packed: one_group(packed, out_weight), group_arguments)
    prefill_out = prefill.reshape(PREFILL_TOKENS, MODEL_WIDTH)
    key_value_pages = jnp.stack([prompt_keys, prompt_values], axis=1).reshape(N_REQ, GROUP_PAGES, PAGE_TOKENS, 2, KEY_VALUE_HEADS * HEAD_SIZE)
    target_group = page_dest[:, :, 0].astype(jnp.int32)
    marks = (target_group[:, :, None] == jnp.arange(N_REQ, dtype=jnp.int32)[None, None, :]).astype(jnp.int32)
    earlier = (jnp.cumsum(marks, axis=1) - marks).astype(jnp.int32)
    in_lane = lax.optimization_barrier(jnp.sum(earlier * marks, axis=2)).astype(jnp.int32)
    page_slot_index = (jnp.arange(N_REQ, dtype=jnp.int32)[:, None] * CAP + in_lane).astype(jnp.int32)
    target_page_store = jnp.zeros((N_REQ, PAGE_SLOTS, PAGE_TOKENS, 2, KEY_VALUE_HEADS * HEAD_SIZE), jnp.bfloat16).at[target_group, page_slot_index].set(key_value_pages)
    return (prefill_out, target_page_store, decoded)
```

```python
import math

import jax
import jax.numpy as jnp
from jax import lax
from jax.experimental import pallas as pl
from jax.experimental.pallas import tpu as pltpu
from jax.sharding import PartitionSpec as P

QUERY_HEADS = 24
KEY_VALUE_HEADS = 8
HEAD_SIZE = 64
PAGE_TOKENS = 8
LONGEST = 512
BLOCK = 256
LANES = 128
DECODE_ROWS = 16

masked_score = -1e30
scale = 1.0 / math.sqrt(HEAD_SIZE)
f32 = jnp.float32
bf16 = jnp.bfloat16


def pair_kernel(k_ref, v_ref, out_ref):
    cols = out_ref.shape[2] // 2
    for c in range(out_ref.shape[0]):
        out_ref[c, :, :cols] = k_ref[:, c * cols : (c + 1) * cols]
        out_ref[c, :, cols:] = v_ref[:, c * cols : (c + 1) * cols]


def split_kernel(place_ref, q_ref, *out_refs):
    n = len(out_refs)
    cols = out_refs[0].shape[1]
    for shift, out_ref in enumerate(out_refs):
        start = pl.multiple_of(lax.rem(place_ref[0] + shift, n) * cols, LANES)
        out_ref[...] = q_ref[:, pl.ds(start, cols)]


def page_kernel(slot_ref, kv_ref, out_ref):
    out_ref[...] = jnp.zeros(out_ref.shape, out_ref.dtype)
    rows = lax.broadcasted_iota(jnp.int32, (2 * LANES, 2 * LANES), 0)
    cols = lax.broadcasted_iota(jnp.int32, (2 * LANES, 2 * LANES), 1)
    weave = (cols == (rows % 2) * LANES + rows // 2).astype(f32).astype(bf16)
    page_rows = 2 * PAGE_TOKENS
    per_chunk = LANES // PAGE_TOKENS
    chunks_per_block = kv_ref.shape[1] // LANES
    for block in range(kv_ref.shape[0]):
        for part in range(chunks_per_block):
            here = pl.ds(part * LANES, LANES)
            both = jnp.concatenate(
                [kv_ref[block, here, :LANES], kv_ref[block, here, LANES:]], axis=0
            )
            woven = jnp.dot(weave, both, preferred_element_type=f32).astype(bf16)
            for p in range(per_chunk):
                page = (block * chunks_per_block + part) * per_chunk + p
                out_ref[slot_ref[page]] = woven[p * page_rows : (p + 1) * page_rows]


def variants(pair, lane):
    wide = pair.astype(f32)
    swapped = pltpu.roll(wide, HEAD_SIZE, 1)
    low = lane < HEAD_SIZE
    zero = jnp.zeros_like(wide)
    return (
        (jnp.where(low, wide, zero), jnp.where(low, zero, swapped)),
        (jnp.where(low, swapped, zero), jnp.where(low, zero, wide)),
    )


def attention_kernel(place_ref, len_ref, *refs):
    n_blocks = (len(refs) - 11) // 2
    q_refs = refs[:n_blocks]
    kv_ref, dq_ref, dk_ref, dv_ref = refs[n_blocks : n_blocks + 4]
    out_refs = refs[n_blocks + 4 : 2 * n_blocks + 4]
    q_ref, out_ref, k_var, v_var, dq_pad, dk_pad, dv_pad = refs[2 * n_blocks + 4 :]
    for pad_ref, given_ref in ((dq_pad, dq_ref), (dk_pad, dk_ref), (dv_pad, dv_ref)):
        pad_ref[...] = jnp.zeros(pad_ref.shape, f32)
        pad_ref[: given_ref.shape[1], :] = given_ref[0].astype(f32)
    place = place_ref[0]
    for shift in range(n_blocks):
        q_ref[lax.rem(place + n_blocks - shift, n_blocks)] = q_refs[shift][...]
    tokens = n_blocks * BLOCK
    end0 = len_ref[0, 0]
    end1 = end0 + len_ref[0, 1]
    heads = q_ref.shape[2] // HEAD_SIZE
    per_kv = QUERY_HEADS // KEY_VALUE_HEADS

    for b in range(n_blocks):
        lane = lax.broadcasted_iota(jnp.int32, (BLOCK, LANES), 1)
        here = pl.ds(b * BLOCK, BLOCK)
        k_all = variants(kv_ref[b, :, :LANES], lane)
        v_all = variants(kv_ref[b, :, LANES:], lane)
        for g in range(2):
            for half in range(2):
                k_var[g, half, here, :] = k_all[g][half].astype(bf16)
                v_var[g, half, here, :] = v_all[g][half].astype(bf16)

    for b in range(n_blocks):
        first = max(0, b - LONGEST // BLOCK)
        keys = (b + 1 - first) * BLOCK
        span = pl.ds(first * BLOCK, keys)
        q_pos = b * BLOCK + lax.broadcasted_iota(jnp.int32, (BLOCK, keys), 0)
        k_pos = first * BLOCK + lax.broadcasted_iota(jnp.int32, (BLOCK, keys), 1)
        begin = jnp.where(q_pos >= end1, end1, jnp.where(q_pos >= end0, end0, 0))
        bias = jnp.where((k_pos <= q_pos) & (k_pos >= begin), 0.0, masked_score).astype(f32)
        lane = lax.broadcasted_iota(jnp.int32, (BLOCK, LANES), 1)
        for pair in range(heads // 2):
            q_pair = q_ref[b, :, pair * LANES : (pair + 1) * LANES] * jnp.asarray(scale, bf16)
            weighted = None
            totals = []
            for half in range(2):
                g = (2 * pair + half) // per_kv
                scores = (
                    lax.dot_general(
                        q_pair, k_var[g, half, span, :], (((1,), (1,)), ((), ())),
                        preferred_element_type=f32,
                    )
                    + bias
                )
                top = jnp.max(scores, axis=1, keepdims=True)
                weights = jnp.exp(scores - top)
                totals.append(jnp.sum(weights, axis=1, keepdims=True))
                part = jnp.dot(
                    weights.astype(bf16), v_var[g, half, span, :], preferred_element_type=f32
                )
                weighted = part if weighted is None else weighted + part
            total = jnp.where(lane < HEAD_SIZE, totals[0], totals[1])
            out_ref[b, :, pair * LANES : (pair + 1) * LANES] = (weighted / total).astype(bf16)

    lane = lax.broadcasted_iota(jnp.int32, (DECODE_ROWS, LANES), 1)
    prompt = lax.broadcasted_iota(jnp.int32, (DECODE_ROWS, tokens), 0)
    token = lax.broadcasted_iota(jnp.int32, (DECODE_ROWS, tokens), 1)
    prompt_of = (token >= end0).astype(jnp.int32) + (token >= end1).astype(jnp.int32)
    bias = jnp.where(prompt == prompt_of, 0.0, masked_score).astype(f32)
    dk_all = variants(dk_pad[...], lane)
    dv_all = variants(dv_pad[...], lane)
    for pair in range(heads // 2):
        q_pair = (dq_pad[:, pair * LANES : (pair + 1) * LANES] * scale).astype(bf16)
        weighted = None
        totals = []
        for half in range(2):
            g = (2 * pair + half) // per_kv
            scores = (
                lax.dot_general(
                    q_pair, k_var[g, half], (((1,), (1,)), ((), ())), preferred_element_type=f32
                )
                + bias
            )
            own = jnp.sum(q_pair.astype(f32) * dk_all[g][half], axis=1, keepdims=True)
            top = jnp.maximum(jnp.max(scores, axis=1, keepdims=True), own)
            weights = jnp.exp(scores - top)
            own_weight = jnp.exp(own - top)
            totals.append(jnp.sum(weights, axis=1, keepdims=True) + own_weight)
            part = (
                jnp.dot(weights.astype(bf16), v_var[g, half], preferred_element_type=f32)
                + own_weight.astype(bf16).astype(f32) * dv_all[g][half]
            )
            weighted = part if weighted is None else weighted + part
        total = jnp.where(lane < HEAD_SIZE, totals[0], totals[1])
        rows = (weighted / total).astype(bf16)
        for result_ref in out_refs:
            result_ref[BLOCK:, pair * LANES : (pair + 1) * LANES] = rows
    for shift, result_ref in enumerate(out_refs):
        result_ref[:BLOCK, :] = out_ref[lax.rem(place + shift, n_blocks)]


def out_kernel(place_ref, core_ref, *refs):
    n = len(refs) - 10
    attn_refs = refs[:n]
    w_ref, beside_ref, across_ref, near_ref, far_ref = refs[n : n + 5]
    res_ref, dres_ref, out_ref, dec_ref, attn_ref = refs[n + 5 :]
    place, core = place_ref[0], core_ref[0]
    width = attn_refs[0].shape[1]
    half = n // 2
    for shift in range(n):
        attn_ref[lax.rem(place + n - shift, n)] = attn_refs[shift][...]

    def project(block, terms):
        start = pl.multiple_of(lax.rem(block, n) * width, LANES)
        total = res_ref[:, pl.ds(start, width)].astype(f32)
        for rows, weight in terms:
            total += jnp.dot(rows, weight, preferred_element_type=f32)
        out_ref[:, pl.ds(start, width)] = total.astype(bf16)

    def whole(ref):
        return [(attn_ref[i, :BLOCK], ref[i * width : (i + 1) * width]) for i in range(n)]

    project(place, whole(w_ref))
    project(place + n - 1 + 2 * core, whole(beside_ref))
    project(place + 1 + 2 * core, whole(across_ref))
    halves = []
    for i in range(half):
        rows = slice(i * width, (i + 1) * width)
        halves.append((attn_ref[core * half + i, :BLOCK], near_ref[rows]))
        halves.append((attn_ref[(1 - core) * half + i, :BLOCK], far_ref[rows]))
    project(place + 2, halves)

    extra = jnp.zeros((DECODE_ROWS, width), f32)
    for i in range(n):
        extra += jnp.dot(
            attn_ref[i, BLOCK:], w_ref[i * width : (i + 1) * width], preferred_element_type=f32
        )
    count = dres_ref.shape[1]
    dec_ref[0] = (dres_ref[0].astype(f32) + extra[:count]).astype(bf16)


def shards(
    prefill_residual,
    prompt_queries,
    prompt_keys,
    prompt_values,
    out_weight,
    prompt_token_counts,
    page_dest,
    decode_residual,
    decoded_queries,
    decoded_keys,
    decoded_values,
):
    n_ctx = lax.axis_size("ctx")
    n_req = lax.axis_size("req")
    rows, width = prompt_queries.shape
    q_cols = width // n_ctx
    kv_cols = prompt_keys.shape[1] // n_ctx
    core = lax.axis_index("req") % 2
    vmem = pl.BlockSpec(memory_space=pltpu.VMEM)
    smem = pl.BlockSpec(memory_space=pltpu.SMEM)

    kv_parts = pl.pallas_call(
        pair_kernel,
        out_shape=jax.ShapeDtypeStruct((n_ctx, rows, 2 * kv_cols), bf16),
        in_specs=[vmem, vmem],
        out_specs=vmem,
        name="pair",
    )(prompt_keys, prompt_values)
    kv = lax.all_to_all(kv_parts, "ctx", 0, 0, tiled=True)
    kv_parts, q_source = lax.optimization_barrier((kv_parts, prompt_queries))
    place = lax.axis_index("ctx").reshape(1)
    send = lambda a, shift: lax.ppermute(a, "ctx", [(i, (i + shift) % n_ctx) for i in range(n_ctx)])
    spread = lambda parts: [parts[0]] + [send(parts[i], i) for i in range(1, n_ctx)]
    q_parts = pl.pallas_call(
        split_kernel,
        out_shape=[jax.ShapeDtypeStruct((rows, q_cols), bf16)] * n_ctx,
        in_specs=[smem, vmem],
        out_specs=[vmem] * n_ctx,
        name="split",
    )(place, q_source)
    q = spread(q_parts)

    pages = page_dest.shape[1]
    dest = page_dest[0, :, 0]
    index = jnp.arange(pages, dtype=jnp.int32)
    lane = jnp.sum(
        ((dest[:, None] == dest[None, :]) & (index[None, :] < index[:, None])).astype(jnp.int32), axis=1
    )
    lane_cap = max(2, 2 * pages // n_req)
    slots, q_parts = lax.optimization_barrier((dest * lane_cap + lane, q_parts))
    outgoing = pl.pallas_call(
        page_kernel,
        out_shape=jax.ShapeDtypeStruct((n_req * lane_cap, 2 * PAGE_TOKENS, kv_cols), bf16),
        in_specs=[smem, vmem],
        out_specs=vmem,
        name="pages",
    )(slots, kv)
    store = lax.all_to_all(outgoing, "req", 0, 0, tiled=True)
    outgoing, w_source, q, kv = lax.optimization_barrier((outgoing, out_weight, q, kv))
    target_page_store = store.reshape(1, n_req * lane_cap, PAGE_TOKENS, 2, kv_cols)

    half_rows = width // 2
    place_of = lambda r, c: r * n_ctx + c % n_ctx
    ring = [
        (place_of(r, c), place_of(r, c + (1 if r % 2 == 0 else -1)))
        for r in range(n_req)
        for c in range(n_ctx)
    ]
    swap = [(r, r ^ 1) for r in range(n_req)]
    w_beside = lax.ppermute(w_source, ("req", "ctx"), ring)

    attention = pl.pallas_call(
        attention_kernel,
        out_shape=[jax.ShapeDtypeStruct((rows + DECODE_ROWS, q_cols), bf16)] * n_ctx,
        in_specs=[smem, smem] + [vmem] * (n_ctx + 4),
        out_specs=[vmem] * n_ctx,
        scratch_shapes=[pltpu.VMEM((n_ctx, rows, q_cols), bf16)] * 2
        + [pltpu.VMEM((2, 2, n_ctx * rows, LANES), bf16)] * 2
        + [pltpu.VMEM((DECODE_ROWS, q_cols), f32)]
        + [pltpu.VMEM((DECODE_ROWS, kv_cols), f32)] * 2,
        name="attend",
    )(place, prompt_token_counts, *q, kv, decoded_queries, decoded_keys, decoded_values)
    back = spread(attention)
    w_beside, attention = lax.optimization_barrier((w_beside, attention))
    w_across = lax.ppermute(w_beside, "req", swap)
    w_near = lax.ppermute(
        lax.dynamic_slice_in_dim(w_beside, core * half_rows, half_rows, 0), ("req", "ctx"), ring
    )
    w_far = lax.ppermute(w_near, "req", swap)

    prefill_out, decode_out = pl.pallas_call(
        out_kernel,
        out_shape=(
            jax.ShapeDtypeStruct(prefill_residual.shape, bf16),
            jax.ShapeDtypeStruct(decode_residual.shape, bf16),
        ),
        in_specs=[smem, smem] + [vmem] * (n_ctx + 7),
        out_specs=(vmem, vmem),
        scratch_shapes=[pltpu.VMEM((n_ctx, rows + DECODE_ROWS, q_cols), bf16)],
        name="project",
    )(
        place,
        core.reshape(1),
        *back,
        out_weight,
        w_beside,
        w_across,
        w_near,
        w_far,
        prefill_residual,
        decode_residual,
    )
    return (prefill_out, target_page_store, decode_out)


def solution(mesh):
    in_specs = (
        P(("req", "ctx"), None),
        P(("req", "ctx"), None),
        P(("req", "ctx"), None),
        P(("req", "ctx"), None),
        P(None, "ctx"),
        P("req", None),
        P("req", None, None),
        P("req", None, "ctx"),
        P("req", None, "ctx"),
        P("req", None, "ctx"),
        P("req", None, "ctx"),
    )
    out_specs = (P(("req", "ctx"), None), P("req", None, None, None, "ctx"), P("req", None, "ctx"))
    return jax.shard_map(shards, mesh=mesh, in_specs=in_specs, out_specs=out_specs, check_vma=False)
```

```python
import math

import jax
import jax.numpy as jnp
from jax import lax
from jax.experimental import pallas as pl
from jax.experimental.pallas import tpu as pltpu
from jax.sharding import PartitionSpec as P

QUERY_HEADS = 24
KEY_VALUE_HEADS = 8
HEAD_SIZE = 64
PAGE_TOKENS = 8
LONGEST = 512
BLOCK = 256
LANES = 128
DECODE_ROWS = 16

masked_score = -1e30
scale = 1.0 / math.sqrt(HEAD_SIZE)
f32 = jnp.float32
bf16 = jnp.bfloat16


def pair_kernel(k_ref, v_ref, out_ref):
    cols = out_ref.shape[2] // 2
    for c in range(out_ref.shape[0]):
        out_ref[c, :, :cols] = k_ref[:, c * cols : (c + 1) * cols]
        out_ref[c, :, cols:] = v_ref[:, c * cols : (c + 1) * cols]


def split_kernel(place_ref, q_ref, *out_refs):
    n = len(out_refs)
    cols = out_refs[0].shape[1]
    for shift, out_ref in enumerate(out_refs):
        start = pl.multiple_of(lax.rem(place_ref[0] + shift, n) * cols, LANES)
        out_ref[...] = q_ref[:, pl.ds(start, cols)]


def page_kernel(slot_ref, kv_ref, out_ref):
    out_ref[...] = jnp.zeros(out_ref.shape, out_ref.dtype)
    rows = lax.broadcasted_iota(jnp.int32, (2 * LANES, 2 * LANES), 0)
    cols = lax.broadcasted_iota(jnp.int32, (2 * LANES, 2 * LANES), 1)
    weave = (cols == (rows % 2) * LANES + rows // 2).astype(f32).astype(bf16)
    page_rows = 2 * PAGE_TOKENS
    per_chunk = LANES // PAGE_TOKENS
    chunks_per_block = kv_ref.shape[1] // LANES
    for block in range(kv_ref.shape[0]):
        for part in range(chunks_per_block):
            here = pl.ds(part * LANES, LANES)
            both = jnp.concatenate(
                [kv_ref[block, here, :LANES], kv_ref[block, here, LANES:]], axis=0
            )
            woven = jnp.dot(weave, both, preferred_element_type=f32).astype(bf16)
            for p in range(per_chunk):
                page = (block * chunks_per_block + part) * per_chunk + p
                out_ref[slot_ref[page]] = woven[p * page_rows : (p + 1) * page_rows]


def variants(pair, lane):
    wide = pair.astype(f32)
    swapped = pltpu.roll(wide, HEAD_SIZE, 1)
    low = lane < HEAD_SIZE
    zero = jnp.zeros_like(wide)
    return (
        (jnp.where(low, wide, zero), jnp.where(low, zero, swapped)),
        (jnp.where(low, swapped, zero), jnp.where(low, zero, wide)),
    )


def attention_kernel(place_ref, len_ref, *refs):
    n_blocks = (len(refs) - 11) // 2
    q_refs = refs[:n_blocks]
    kv_ref, dq_ref, dk_ref, dv_ref = refs[n_blocks : n_blocks + 4]
    out_refs = refs[n_blocks + 4 : 2 * n_blocks + 4]
    q_ref, out_ref, k_var, v_var, dq_pad, dk_pad, dv_pad = refs[2 * n_blocks + 4 :]
    for pad_ref, given_ref in ((dq_pad, dq_ref), (dk_pad, dk_ref), (dv_pad, dv_ref)):
        pad_ref[...] = jnp.zeros(pad_ref.shape, f32)
        pad_ref[: given_ref.shape[1], :] = given_ref[0].astype(f32)
    place = place_ref[0]
    for shift in range(n_blocks):
        q_ref[lax.rem(place + n_blocks - shift, n_blocks)] = q_refs[shift][...]
    tokens = n_blocks * BLOCK
    end0 = len_ref[0, 0]
    end1 = end0 + len_ref[0, 1]
    heads = q_ref.shape[2] // HEAD_SIZE
    per_kv = QUERY_HEADS // KEY_VALUE_HEADS

    for b in range(n_blocks):
        lane = lax.broadcasted_iota(jnp.int32, (BLOCK, LANES), 1)
        here = pl.ds(b * BLOCK, BLOCK)
        k_all = variants(kv_ref[b, :, :LANES], lane)
        v_all = variants(kv_ref[b, :, LANES:], lane)
        for g in range(2):
            for half in range(2):
                k_var[g, half, here, :] = k_all[g][half].astype(bf16)
                v_var[g, half, here, :] = v_all[g][half].astype(bf16)

    for b in range(n_blocks):
        first = max(0, b - LONGEST // BLOCK)
        keys = (b + 1 - first) * BLOCK
        span = pl.ds(first * BLOCK, keys)
        q_pos = b * BLOCK + lax.broadcasted_iota(jnp.int32, (BLOCK, keys), 0)
        k_pos = first * BLOCK + lax.broadcasted_iota(jnp.int32, (BLOCK, keys), 1)
        begin = jnp.where(q_pos >= end1, end1, jnp.where(q_pos >= end0, end0, 0))
        bias = jnp.where((k_pos <= q_pos) & (k_pos >= begin), 0.0, masked_score).astype(f32)
        lane = lax.broadcasted_iota(jnp.int32, (BLOCK, LANES), 1)
        for pair in range(heads // 2):
            q_pair = q_ref[b, :, pair * LANES : (pair + 1) * LANES] * jnp.asarray(scale, bf16)
            weighted = None
            totals = []
            for half in range(2):
                g = (2 * pair + half) // per_kv
                scores = (
                    lax.dot_general(
                        q_pair, k_var[g, half, span, :], (((1,), (1,)), ((), ())),
                        preferred_element_type=f32,
                    )
                    + bias
                )
                top = jnp.max(scores, axis=1, keepdims=True)
                weights = jnp.exp(scores - top)
                totals.append(jnp.sum(weights, axis=1, keepdims=True))
                part = jnp.dot(
                    weights.astype(bf16), v_var[g, half, span, :], preferred_element_type=f32
                )
                weighted = part if weighted is None else weighted + part
            total = jnp.where(lane < HEAD_SIZE, totals[0], totals[1])
            out_ref[b, :, pair * LANES : (pair + 1) * LANES] = (weighted / total).astype(bf16)

    lane = lax.broadcasted_iota(jnp.int32, (DECODE_ROWS, LANES), 1)
    prompt = lax.broadcasted_iota(jnp.int32, (DECODE_ROWS, tokens), 0)
    token = lax.broadcasted_iota(jnp.int32, (DECODE_ROWS, tokens), 1)
    prompt_of = (token >= end0).astype(jnp.int32) + (token >= end1).astype(jnp.int32)
    bias = jnp.where(prompt == prompt_of, 0.0, masked_score).astype(f32)
    dk_all = variants(dk_pad[...], lane)
    dv_all = variants(dv_pad[...], lane)
    for pair in range(heads // 2):
        q_pair = (dq_pad[:, pair * LANES : (pair + 1) * LANES] * scale).astype(bf16)
        weighted = None
        totals = []
        for half in range(2):
            g = (2 * pair + half) // per_kv
            scores = (
                lax.dot_general(
                    q_pair, k_var[g, half], (((1,), (1,)), ((), ())), preferred_element_type=f32
                )
                + bias
            )
            own = jnp.sum(q_pair.astype(f32) * dk_all[g][half], axis=1, keepdims=True)
            top = jnp.maximum(jnp.max(scores, axis=1, keepdims=True), own)
            weights = jnp.exp(scores - top)
            own_weight = jnp.exp(own - top)
            totals.append(jnp.sum(weights, axis=1, keepdims=True) + own_weight)
            part = (
                jnp.dot(weights.astype(bf16), v_var[g, half], preferred_element_type=f32)
                + own_weight.astype(bf16).astype(f32) * dv_all[g][half]
            )
            weighted = part if weighted is None else weighted + part
        total = jnp.where(lane < HEAD_SIZE, totals[0], totals[1])
        rows = (weighted / total).astype(bf16)
        for result_ref in out_refs:
            result_ref[BLOCK:, pair * LANES : (pair + 1) * LANES] = rows
    for shift, result_ref in enumerate(out_refs):
        result_ref[:BLOCK, :] = out_ref[lax.rem(place + shift, n_blocks)]


def out_kernel(place_ref, core_ref, *refs):
    n = len(refs) - 13
    attn_refs = refs[:n]
    w_refs = refs[n : n + 4]
    res_hbm, dres_ref, out_ref, dec_ref, attn_ref, w_all, res_ref, w_sems, res_sem = refs[n + 4 :]
    place, core = place_ref[0], core_ref[0]
    width = attn_refs[0].shape[1]
    fetches = [
        pltpu.make_async_copy(w_ref, w_all.at[i], w_sems.at[i]) for i, w_ref in enumerate(w_refs)
    ]
    residual = pltpu.make_async_copy(res_hbm, res_ref, res_sem)
    fetches[0].start()
    residual.start()
    for fetch in fetches[1:]:
        fetch.start()
    for shift in range(n):
        attn_ref[lax.rem(place + n - shift, n)] = attn_refs[shift][...]
    blocks = (place, place + n - 1 + 2 * core, place + 1 + 2 * core, place + 2)
    for i, block in enumerate(blocks):
        fetches[i].wait()
        if i == 0:
            residual.wait()
        start = pl.multiple_of(lax.rem(block, n) * width, LANES)
        total = res_ref[:, pl.ds(start, width)].astype(f32)
        for h in range(n):
            total += jnp.dot(
                attn_ref[h, :BLOCK],
                w_all[i, h * width : (h + 1) * width, :],
                preferred_element_type=f32,
            )
        out_ref[:, pl.ds(start, width)] = total.astype(bf16)
        if i == 0:
            extra = jnp.zeros((DECODE_ROWS, width), f32)
            for h in range(n):
                extra += jnp.dot(
                    attn_ref[h, BLOCK:],
                    w_all[0, h * width : (h + 1) * width, :],
                    preferred_element_type=f32,
                )
            count = dres_ref.shape[1]
            dec_ref[0] = (dres_ref[0].astype(f32) + extra[:count]).astype(bf16)


def shards(
    prefill_residual,
    prompt_queries,
    prompt_keys,
    prompt_values,
    out_weight,
    prompt_token_counts,
    page_dest,
    decode_residual,
    decoded_queries,
    decoded_keys,
    decoded_values,
):
    n_ctx = lax.axis_size("ctx")
    n_req = lax.axis_size("req")
    rows, width = prompt_queries.shape
    q_cols = width // n_ctx
    kv_cols = prompt_keys.shape[1] // n_ctx
    core = lax.axis_index("req") % 2
    vmem = pl.BlockSpec(memory_space=pltpu.VMEM)
    smem = pl.BlockSpec(memory_space=pltpu.SMEM)
    anywhere = pl.BlockSpec(memory_space=pl.ANY)
    near = lambda a: pltpu.with_memory_space_constraint(a, pltpu.VMEM)

    kv_parts = pl.pallas_call(
        pair_kernel,
        out_shape=jax.ShapeDtypeStruct((n_ctx, rows, 2 * kv_cols), bf16),
        in_specs=[vmem, vmem],
        out_specs=vmem,
        name="pair",
    )(prompt_keys, prompt_values)
    kv = lax.all_to_all(kv_parts, "ctx", 0, 0, tiled=True)
    kv_parts, q_source, w_source = lax.optimization_barrier((kv_parts, prompt_queries, out_weight))
    place = lax.axis_index("ctx").reshape(1)
    send = lambda a, shift: lax.ppermute(a, "ctx", [(i, (i + shift) % n_ctx) for i in range(n_ctx)])
    spread = lambda parts: [parts[0]] + [send(parts[i], i) for i in range(1, n_ctx)]
    q_parts = pl.pallas_call(
        split_kernel,
        out_shape=[jax.ShapeDtypeStruct((rows, q_cols), bf16)] * n_ctx,
        in_specs=[smem, vmem],
        out_specs=[vmem] * n_ctx,
        name="split",
    )(place, q_source)

    place_of = lambda r, c: r * n_ctx + c % n_ctx
    ring = [
        (place_of(r, c), place_of(r, c + (1 if r % 2 == 0 else -1)))
        for r in range(n_req)
        for c in range(n_ctx)
    ]
    swap = [(r, r ^ 1) for r in range(n_req)]

    pages = page_dest.shape[1]
    dest = page_dest[0, :, 0]
    index = jnp.arange(pages, dtype=jnp.int32)
    lane = jnp.sum(
        ((dest[:, None] == dest[None, :]) & (index[None, :] < index[:, None])).astype(jnp.int32), axis=1
    )
    lane_cap = max(2, 2 * pages // n_req)
    slots, q_parts = lax.optimization_barrier((dest * lane_cap + lane, q_parts))
    outgoing = pl.pallas_call(
        page_kernel,
        out_shape=jax.ShapeDtypeStruct((n_req * lane_cap, 2 * PAGE_TOKENS, kv_cols), bf16),
        in_specs=[smem, vmem],
        out_specs=vmem,
        name="pages",
    )(slots, near(kv))
    store = lax.all_to_all(outgoing, "req", 0, 0, tiled=True)
    w_beside = lax.ppermute(w_source, ("req", "ctx"), ring)
    outgoing, w_beside = lax.optimization_barrier((outgoing, w_beside))
    w_beside, q_parts = lax.optimization_barrier((w_beside, q_parts))
    q = spread(q_parts)
    target_page_store = store.reshape(1, n_req * lane_cap, PAGE_TOKENS, 2, kv_cols)

    w_across = lax.ppermute(w_beside, "req", swap)
    w_beyond = lax.ppermute(w_beside, ("req", "ctx"), ring)

    attention = pl.pallas_call(
        attention_kernel,
        out_shape=[jax.ShapeDtypeStruct((rows + DECODE_ROWS, q_cols), bf16)] * n_ctx,
        in_specs=[smem, smem] + [vmem] * (n_ctx + 4),
        out_specs=[vmem] * n_ctx,
        scratch_shapes=[pltpu.VMEM((n_ctx, rows, q_cols), bf16)] * 2
        + [pltpu.VMEM((2, 2, n_ctx * rows, LANES), bf16)] * 2
        + [pltpu.VMEM((DECODE_ROWS, q_cols), f32)]
        + [pltpu.VMEM((DECODE_ROWS, kv_cols), f32)] * 2,
        name="attend",
        cost_estimate=pl.CostEstimate(flops=30000000000, transcendentals=0, bytes_accessed=0),
    )(place, prompt_token_counts, q[0], *map(near, q[1:]), near(kv), decoded_queries, decoded_keys, decoded_values)
    back = spread(attention)
    prefill_out, decode_out = pl.pallas_call(
        out_kernel,
        out_shape=(
            jax.ShapeDtypeStruct(prefill_residual.shape, bf16),
            jax.ShapeDtypeStruct(decode_residual.shape, bf16),
        ),
        in_specs=[smem, smem] + [vmem] * n_ctx + [anywhere] * 5 + [vmem],
        out_specs=(vmem, vmem),
        scratch_shapes=[
            pltpu.VMEM((n_ctx, rows + DECODE_ROWS, q_cols), bf16),
            pltpu.VMEM((n_ctx, width, q_cols), bf16),
            pltpu.VMEM((rows, width), bf16),
            pltpu.SemaphoreType.DMA((n_ctx,)),
            pltpu.SemaphoreType.DMA,
        ],
        name="project",
    )(
        place,
        core.reshape(1),
        back[0],
        *map(near, back[1:]),
        out_weight,
        w_beside,
        w_across,
        w_beyond,
        prefill_residual,
        decode_residual,
    )
    return (prefill_out, target_page_store, decode_out)


def solution(mesh):
    in_specs = (
        P(("req", "ctx"), None),
        P(("req", "ctx"), None),
        P(("req", "ctx"), None),
        P(("req", "ctx"), None),
        P(None, "ctx"),
        P("req", None),
        P("req", None, None),
        P("req", None, "ctx"),
        P("req", None, "ctx"),
        P("req", None, "ctx"),
        P("req", None, "ctx"),
    )
    out_specs = (P(("req", "ctx"), None), P("req", None, None, None, "ctx"), P("req", None, "ctx"))
    return jax.shard_map(shards, mesh=mesh, in_specs=in_specs, out_specs=out_specs, check_vma=False)
```

```python
import math

import jax
import jax.numpy as jnp
from jax import lax
from jax.experimental import pallas as pl
from jax.experimental.pallas import tpu as pltpu
from jax.sharding import PartitionSpec as P

QUERY_HEADS = 24
KEY_VALUE_HEADS = 8
HEAD_SIZE = 64
PAGE_TOKENS = 8
LONGEST = 512
BLOCK = 256
LANES = 128
DECODE_ROWS = 16

masked_score = -1e30
scale = 1.0 / math.sqrt(HEAD_SIZE)
f32 = jnp.float32
bf16 = jnp.bfloat16


def pair_kernel(k_ref, v_ref, out_ref):
    cols = out_ref.shape[2] // 2
    for c in range(out_ref.shape[0]):
        out_ref[c, :, :cols] = k_ref[:, c * cols : (c + 1) * cols]
        out_ref[c, :, cols:] = v_ref[:, c * cols : (c + 1) * cols]


def split_kernel(place_ref, q_ref, *out_refs):
    n = len(out_refs)
    cols = out_refs[0].shape[1]
    for shift, out_ref in enumerate(out_refs):
        start = pl.multiple_of(lax.rem(place_ref[0] + shift, n) * cols, LANES)
        out_ref[...] = q_ref[:, pl.ds(start, cols)]


def page_kernel(slot_ref, kv_ref, out_ref):
    out_ref[...] = jnp.zeros(out_ref.shape, out_ref.dtype)
    rows = lax.broadcasted_iota(jnp.int32, (2 * LANES, 2 * LANES), 0)
    cols = lax.broadcasted_iota(jnp.int32, (2 * LANES, 2 * LANES), 1)
    weave = (cols == (rows % 2) * LANES + rows // 2).astype(f32).astype(bf16)
    page_rows = 2 * PAGE_TOKENS
    per_chunk = LANES // PAGE_TOKENS
    chunks_per_block = kv_ref.shape[1] // LANES
    for block in range(kv_ref.shape[0]):
        for part in range(chunks_per_block):
            here = pl.ds(part * LANES, LANES)
            both = jnp.concatenate(
                [kv_ref[block, here, :LANES], kv_ref[block, here, LANES:]], axis=0
            )
            woven = jnp.dot(weave, both, preferred_element_type=f32).astype(bf16)
            for p in range(per_chunk):
                page = (block * chunks_per_block + part) * per_chunk + p
                out_ref[slot_ref[page]] = woven[p * page_rows : (p + 1) * page_rows]


def variants(pair, lane):
    wide = pair.astype(f32)
    swapped = pltpu.roll(wide, HEAD_SIZE, 1)
    low = lane < HEAD_SIZE
    zero = jnp.zeros_like(wide)
    return (
        (jnp.where(low, wide, zero), jnp.where(low, zero, swapped)),
        (jnp.where(low, swapped, zero), jnp.where(low, zero, wide)),
    )


def attention_kernel(place_ref, len_ref, *refs):
    n_blocks = (len(refs) - 11) // 2
    q_refs = refs[:n_blocks]
    kv_ref, dq_ref, dk_ref, dv_ref = refs[n_blocks : n_blocks + 4]
    out_refs = refs[n_blocks + 4 : 2 * n_blocks + 4]
    q_ref, out_ref, k_var, v_var, dq_pad, dk_pad, dv_pad = refs[2 * n_blocks + 4 :]
    for pad_ref, given_ref in ((dq_pad, dq_ref), (dk_pad, dk_ref), (dv_pad, dv_ref)):
        pad_ref[...] = jnp.zeros(pad_ref.shape, f32)
        pad_ref[: given_ref.shape[1], :] = given_ref[0].astype(f32)
    place = place_ref[0]
    for shift in range(n_blocks):
        q_ref[lax.rem(place + n_blocks - shift, n_blocks)] = q_refs[shift][...]
    tokens = n_blocks * BLOCK
    end0 = len_ref[0, 0]
    end1 = end0 + len_ref[0, 1]
    heads = q_ref.shape[2] // HEAD_SIZE
    per_kv = QUERY_HEADS // KEY_VALUE_HEADS

    for b in range(n_blocks):
        lane = lax.broadcasted_iota(jnp.int32, (BLOCK, LANES), 1)
        here = pl.ds(b * BLOCK, BLOCK)
        k_all = variants(kv_ref[b, :, :LANES], lane)
        v_all = variants(kv_ref[b, :, LANES:], lane)
        for g in range(2):
            for half in range(2):
                k_var[g, half, here, :] = k_all[g][half].astype(bf16)
                v_var[g, half, here, :] = v_all[g][half].astype(bf16)

    for b in range(n_blocks):
        first = max(0, b - LONGEST // BLOCK)
        keys = (b + 1 - first) * BLOCK
        span = pl.ds(first * BLOCK, keys)
        q_pos = b * BLOCK + lax.broadcasted_iota(jnp.int32, (BLOCK, keys), 0)
        k_pos = first * BLOCK + lax.broadcasted_iota(jnp.int32, (BLOCK, keys), 1)
        begin = jnp.where(q_pos >= end1, end1, jnp.where(q_pos >= end0, end0, 0))
        bias = jnp.where((k_pos <= q_pos) & (k_pos >= begin), 0.0, masked_score).astype(f32)
        lane = lax.broadcasted_iota(jnp.int32, (BLOCK, LANES), 1)
        for pair in range(heads // 2):
            q_pair = q_ref[b, :, pair * LANES : (pair + 1) * LANES] * jnp.asarray(scale, bf16)
            weighted = None
            totals = []
            for half in range(2):
                g = (2 * pair + half) // per_kv
                scores = (
                    lax.dot_general(
                        q_pair, k_var[g, half, span, :], (((1,), (1,)), ((), ())),
                        preferred_element_type=f32,
                    )
                    + bias
                )
                top = jnp.max(scores, axis=1, keepdims=True)
                weights = jnp.exp(scores - top)
                totals.append(jnp.sum(weights, axis=1, keepdims=True))
                part = jnp.dot(
                    weights.astype(bf16), v_var[g, half, span, :], preferred_element_type=f32
                )
                weighted = part if weighted is None else weighted + part
            total = jnp.where(lane < HEAD_SIZE, totals[0], totals[1])
            out_ref[b, :, pair * LANES : (pair + 1) * LANES] = (weighted / total).astype(bf16)

    lane = lax.broadcasted_iota(jnp.int32, (DECODE_ROWS, LANES), 1)
    prompt = lax.broadcasted_iota(jnp.int32, (DECODE_ROWS, tokens), 0)
    token = lax.broadcasted_iota(jnp.int32, (DECODE_ROWS, tokens), 1)
    prompt_of = (token >= end0).astype(jnp.int32) + (token >= end1).astype(jnp.int32)
    bias = jnp.where(prompt == prompt_of, 0.0, masked_score).astype(f32)
    dk_all = variants(dk_pad[...], lane)
    dv_all = variants(dv_pad[...], lane)
    for pair in range(heads // 2):
        q_pair = (dq_pad[:, pair * LANES : (pair + 1) * LANES] * scale).astype(bf16)
        weighted = None
        totals = []
        for half in range(2):
            g = (2 * pair + half) // per_kv
            scores = (
                lax.dot_general(
                    q_pair, k_var[g, half], (((1,), (1,)), ((), ())), preferred_element_type=f32
                )
                + bias
            )
            own = jnp.sum(q_pair.astype(f32) * dk_all[g][half], axis=1, keepdims=True)
            top = jnp.maximum(jnp.max(scores, axis=1, keepdims=True), own)
            weights = jnp.exp(scores - top)
            own_weight = jnp.exp(own - top)
            totals.append(jnp.sum(weights, axis=1, keepdims=True) + own_weight)
            part = (
                jnp.dot(weights.astype(bf16), v_var[g, half], preferred_element_type=f32)
                + own_weight.astype(bf16).astype(f32) * dv_all[g][half]
            )
            weighted = part if weighted is None else weighted + part
        total = jnp.where(lane < HEAD_SIZE, totals[0], totals[1])
        rows = (weighted / total).astype(bf16)
        for result_ref in out_refs:
            result_ref[BLOCK:, pair * LANES : (pair + 1) * LANES] = rows
    for shift, result_ref in enumerate(out_refs):
        result_ref[:BLOCK, :] = out_ref[lax.rem(place + shift, n_blocks)]


def out_kernel(place_ref, core_ref, *refs):
    n = len(refs) - 9
    attn_refs, w_refs = refs[:n], refs[n : n + 4]
    res_ref, dres_ref, out_ref, dec_ref, attn_ref = refs[n + 4 :]
    place, core = place_ref[0], core_ref[0]
    width = attn_refs[0].shape[1]
    for shift in range(n):
        attn_ref[lax.rem(place + n - shift, n)] = attn_refs[shift][...]

    def times(rows, w_ref):
        total = None
        for h in range(n):
            weight = w_ref[h * width : (h + 1) * width, :]
            part = jnp.dot(attn_ref[h, rows], weight, preferred_element_type=f32)
            total = part if total is None else total + part
        return total

    blocks = (place, place + n - 1 + 2 * core, place + 1 + 2 * core, place + 2)
    for w_ref, block in zip(w_refs, blocks):
        start = pl.multiple_of(lax.rem(block, n) * width, LANES)
        residual = res_ref[:, pl.ds(start, width)].astype(f32)
        out_ref[:, pl.ds(start, width)] = (residual + times(slice(0, BLOCK), w_ref)).astype(bf16)
    count = dres_ref.shape[1]
    extra = times(slice(BLOCK, BLOCK + DECODE_ROWS), w_refs[0])
    dec_ref[0] = (dres_ref[0].astype(f32) + extra[:count]).astype(bf16)


def shards(
    prefill_residual,
    prompt_queries,
    prompt_keys,
    prompt_values,
    out_weight,
    prompt_token_counts,
    page_dest,
    decode_residual,
    decoded_queries,
    decoded_keys,
    decoded_values,
):
    n_ctx = lax.axis_size("ctx")
    n_req = lax.axis_size("req")
    rows, width = prompt_queries.shape
    q_cols = width // n_ctx
    kv_cols = prompt_keys.shape[1] // n_ctx
    core = lax.axis_index("req") % 2
    vmem = pl.BlockSpec(memory_space=pltpu.VMEM)
    smem = pl.BlockSpec(memory_space=pltpu.SMEM)
    near = lambda a: pltpu.with_memory_space_constraint(a, pltpu.VMEM)

    kv_parts = pl.pallas_call(
        pair_kernel,
        out_shape=jax.ShapeDtypeStruct((n_ctx, rows, 2 * kv_cols), bf16),
        in_specs=[vmem, vmem],
        out_specs=vmem,
        name="pair",
    )(prompt_keys, prompt_values)
    kv = lax.all_to_all(kv_parts, "ctx", 0, 0, tiled=True)
    kv_parts, q_source, w_source = lax.optimization_barrier((kv_parts, prompt_queries, out_weight))
    place = lax.axis_index("ctx").reshape(1)
    send = lambda a, shift: lax.ppermute(a, "ctx", [(i, (i + shift) % n_ctx) for i in range(n_ctx)])
    spread = lambda parts: [parts[0]] + [send(parts[i], i) for i in range(1, n_ctx)]
    q_parts = pl.pallas_call(
        split_kernel,
        out_shape=[jax.ShapeDtypeStruct((rows, q_cols), bf16)] * n_ctx,
        in_specs=[smem, vmem],
        out_specs=[vmem] * n_ctx,
        name="split",
    )(place, q_source)

    place_of = lambda r, c: r * n_ctx + c % n_ctx
    ring = [
        (place_of(r, c), place_of(r, c + (1 if r % 2 == 0 else -1)))
        for r in range(n_req)
        for c in range(n_ctx)
    ]
    swap = [(r, r ^ 1) for r in range(n_req)]

    pages = page_dest.shape[1]
    dest = page_dest[0, :, 0]
    index = jnp.arange(pages, dtype=jnp.int32)
    lane = jnp.sum(
        ((dest[:, None] == dest[None, :]) & (index[None, :] < index[:, None])).astype(jnp.int32), axis=1
    )
    lane_cap = max(2, 2 * pages // n_req)
    slots, q_parts = lax.optimization_barrier((dest * lane_cap + lane, q_parts))
    outgoing = pl.pallas_call(
        page_kernel,
        out_shape=jax.ShapeDtypeStruct((n_req * lane_cap, 2 * PAGE_TOKENS, kv_cols), bf16),
        in_specs=[smem, vmem],
        out_specs=vmem,
        name="pages",
    )(slots, near(kv))
    store = lax.all_to_all(outgoing, "req", 0, 0, tiled=True)
    w_beside = lax.ppermute(w_source, ("req", "ctx"), ring)
    outgoing, w_beside = lax.optimization_barrier((outgoing, w_beside))
    w_beside, q_parts = lax.optimization_barrier((w_beside, q_parts))
    q = spread(q_parts)
    target_page_store = store.reshape(1, n_req * lane_cap, PAGE_TOKENS, 2, kv_cols)

    w_across = lax.ppermute(w_beside, "req", swap)
    w_beyond = lax.ppermute(w_beside, ("req", "ctx"), ring)

    attention = pl.pallas_call(
        attention_kernel,
        out_shape=[jax.ShapeDtypeStruct((rows + DECODE_ROWS, q_cols), bf16)] * n_ctx,
        in_specs=[smem, smem] + [vmem] * (n_ctx + 4),
        out_specs=[vmem] * n_ctx,
        scratch_shapes=[pltpu.VMEM((n_ctx, rows, q_cols), bf16)] * 2
        + [pltpu.VMEM((2, 2, n_ctx * rows, LANES), bf16)] * 2
        + [pltpu.VMEM((DECODE_ROWS, q_cols), f32)]
        + [pltpu.VMEM((DECODE_ROWS, kv_cols), f32)] * 2,
        name="attend",
        cost_estimate=pl.CostEstimate(flops=30000000000, transcendentals=0, bytes_accessed=0),
    )(place, prompt_token_counts, q[0], *map(near, q[1:]), near(kv), decoded_queries, decoded_keys, decoded_values)
    back = spread(attention)
    prefill_out, decode_out = pl.pallas_call(
        out_kernel,
        out_shape=(
            jax.ShapeDtypeStruct(prefill_residual.shape, bf16),
            jax.ShapeDtypeStruct(decode_residual.shape, bf16),
        ),
        in_specs=[smem, smem] + [vmem] * (n_ctx + 6),
        out_specs=(vmem, vmem),
        scratch_shapes=[
            pltpu.VMEM((n_ctx, rows + DECODE_ROWS, q_cols), bf16),
        ],
        name="project",
    )(
        place,
        core.reshape(1),
        back[0],
        *map(near, back[1:]),
        out_weight,
        w_beside,
        w_across,
        w_beyond,
        prefill_residual,
        decode_residual,
    )
    return (prefill_out, target_page_store, decode_out)


def solution(mesh):
    in_specs = (
        P(("req", "ctx"), None),
        P(("req", "ctx"), None),
        P(("req", "ctx"), None),
        P(("req", "ctx"), None),
        P(None, "ctx"),
        P("req", None),
        P("req", None, None),
        P("req", None, "ctx"),
        P("req", None, "ctx"),
        P("req", None, "ctx"),
        P("req", None, "ctx"),
    )
    out_specs = (P(("req", "ctx"), None), P("req", None, None, None, "ctx"), P("req", None, "ctx"))
    return jax.shard_map(shards, mesh=mesh, in_specs=in_specs, out_specs=out_specs, check_vma=False)
```

```python
import math

import jax
import jax.numpy as jnp
from jax import lax
from jax.experimental import pallas as pl
from jax.experimental.pallas import tpu as pltpu
from jax.sharding import PartitionSpec as P

QUERY_HEADS = 24
KEY_VALUE_HEADS = 8
HEAD_SIZE = 64
PAGE_TOKENS = 8
LONGEST = 512
BLOCK = 256
LANES = 128
DECODE_ROWS = 16

masked_score = -1e30
scale = 1.0 / math.sqrt(HEAD_SIZE)
f32 = jnp.float32
bf16 = jnp.bfloat16


def pair_kernel(k_ref, v_ref, out_ref):
    cols = out_ref.shape[2] // 2
    for c in range(out_ref.shape[0]):
        out_ref[c, :, :cols] = k_ref[:, c * cols : (c + 1) * cols]
        out_ref[c, :, cols:] = v_ref[:, c * cols : (c + 1) * cols]


def split_kernel(place_ref, q_ref, *out_refs):
    n = len(out_refs)
    cols = out_refs[0].shape[1]
    for shift, out_ref in enumerate(out_refs):
        start = pl.multiple_of(lax.rem(place_ref[0] + shift, n) * cols, LANES)
        out_ref[...] = q_ref[:, pl.ds(start, cols)]


def page_kernel(slot_ref, kv_ref, out_ref):
    out_ref[...] = jnp.zeros(out_ref.shape, out_ref.dtype)
    chunk = LANES // 2
    rows = lax.broadcasted_iota(jnp.int32, (2 * chunk, 2 * chunk), 0)
    cols = lax.broadcasted_iota(jnp.int32, (2 * chunk, 2 * chunk), 1)
    weave = (cols == (rows % 2) * chunk + rows // 2).astype(f32).astype(bf16)
    page_rows = 2 * PAGE_TOKENS
    per_chunk = chunk // PAGE_TOKENS
    sides = [
        jnp.concatenate(
            [
                kv_ref[block, part * chunk : (part + 1) * chunk, :LANES],
                kv_ref[block, part * chunk : (part + 1) * chunk, LANES:],
            ],
            axis=0,
        )
        for block in range(kv_ref.shape[0])
        for part in range(kv_ref.shape[1] // chunk)
    ]
    woven = jnp.dot(weave, jnp.concatenate(sides, axis=1), preferred_element_type=f32).astype(bf16)
    for i in range(len(sides)):
        for p in range(per_chunk):
            out_ref[slot_ref[i * per_chunk + p]] = woven[
                p * page_rows : (p + 1) * page_rows, i * LANES : (i + 1) * LANES
            ]


def variants(pair, lane):
    wide = pair.astype(f32)
    swapped = pltpu.roll(wide, HEAD_SIZE, 1)
    low = lane < HEAD_SIZE
    zero = jnp.zeros_like(wide)
    return (
        (jnp.where(low, wide, zero), jnp.where(low, zero, swapped)),
        (jnp.where(low, swapped, zero), jnp.where(low, zero, wide)),
    )


def attention_kernel(place_ref, len_ref, *refs):
    n_blocks = (len(refs) - 11) // 2
    q_refs = refs[:n_blocks]
    kv_ref, dq_ref, dk_ref, dv_ref = refs[n_blocks : n_blocks + 4]
    out_refs = refs[n_blocks + 4 : 2 * n_blocks + 4]
    q_ref, out_ref, k_var, v_var, dq_pad, dk_pad, dv_pad = refs[2 * n_blocks + 4 :]
    for pad_ref, given_ref in ((dq_pad, dq_ref), (dk_pad, dk_ref), (dv_pad, dv_ref)):
        pad_ref[...] = jnp.zeros(pad_ref.shape, f32)
        pad_ref[: given_ref.shape[1], :] = given_ref[0].astype(f32)
    place = place_ref[0]
    for shift in range(n_blocks):
        q_ref[lax.rem(place + n_blocks - shift, n_blocks)] = q_refs[shift][...]
    tokens = n_blocks * BLOCK
    end0 = len_ref[0, 0]
    end1 = end0 + len_ref[0, 1]
    heads = q_ref.shape[2] // HEAD_SIZE
    per_kv = QUERY_HEADS // KEY_VALUE_HEADS

    for b in range(n_blocks):
        lane = lax.broadcasted_iota(jnp.int32, (BLOCK, LANES), 1)
        here = pl.ds(b * BLOCK, BLOCK)
        k_all = variants(kv_ref[b, :, :LANES], lane)
        v_all = variants(kv_ref[b, :, LANES:], lane)
        for g in range(2):
            for half in range(2):
                k_var[g, half, here, :] = k_all[g][half].astype(bf16)
                v_var[g, half, here, :] = v_all[g][half].astype(bf16)

    for b in range(n_blocks):
        first = max(0, b - LONGEST // BLOCK)
        keys = (b + 1 - first) * BLOCK
        span = pl.ds(first * BLOCK, keys)
        q_pos = b * BLOCK + lax.broadcasted_iota(jnp.int32, (BLOCK, keys), 0)
        k_pos = first * BLOCK + lax.broadcasted_iota(jnp.int32, (BLOCK, keys), 1)
        begin = jnp.where(q_pos >= end1, end1, jnp.where(q_pos >= end0, end0, 0))
        bias = jnp.where((k_pos <= q_pos) & (k_pos >= begin), 0.0, masked_score).astype(f32)
        lane = lax.broadcasted_iota(jnp.int32, (BLOCK, LANES), 1)
        for pair in range(heads // 2):
            q_pair = q_ref[b, :, pair * LANES : (pair + 1) * LANES] * jnp.asarray(scale, bf16)
            weighted = None
            totals = []
            for half in range(2):
                g = (2 * pair + half) // per_kv
                scores = (
                    lax.dot_general(
                        q_pair, k_var[g, half, span, :], (((1,), (1,)), ((), ())),
                        preferred_element_type=f32,
                    )
                    + bias
                )
                top = jnp.max(scores, axis=1, keepdims=True)
                weights = jnp.exp(scores - top)
                totals.append(jnp.sum(weights, axis=1, keepdims=True))
                part = jnp.dot(
                    weights.astype(bf16), v_var[g, half, span, :], preferred_element_type=f32
                )
                weighted = part if weighted is None else weighted + part
            total = jnp.where(lane < HEAD_SIZE, totals[0], totals[1])
            out_ref[b, :, pair * LANES : (pair + 1) * LANES] = (weighted / total).astype(bf16)

    lane = lax.broadcasted_iota(jnp.int32, (DECODE_ROWS, LANES), 1)
    prompt = lax.broadcasted_iota(jnp.int32, (DECODE_ROWS, tokens), 0)
    token = lax.broadcasted_iota(jnp.int32, (DECODE_ROWS, tokens), 1)
    prompt_of = (token >= end0).astype(jnp.int32) + (token >= end1).astype(jnp.int32)
    bias = jnp.where(prompt == prompt_of, 0.0, masked_score).astype(f32)
    dk_all = variants(dk_pad[...], lane)
    dv_all = variants(dv_pad[...], lane)
    for pair in range(heads // 2):
        q_pair = (dq_pad[:, pair * LANES : (pair + 1) * LANES] * scale).astype(bf16)
        weighted = None
        totals = []
        for half in range(2):
            g = (2 * pair + half) // per_kv
            scores = (
                lax.dot_general(
                    q_pair, k_var[g, half], (((1,), (1,)), ((), ())), preferred_element_type=f32
                )
                + bias
            )
            own = jnp.sum(q_pair.astype(f32) * dk_all[g][half], axis=1, keepdims=True)
            top = jnp.maximum(jnp.max(scores, axis=1, keepdims=True), own)
            weights = jnp.exp(scores - top)
            own_weight = jnp.exp(own - top)
            totals.append(jnp.sum(weights, axis=1, keepdims=True) + own_weight)
            part = (
                jnp.dot(weights.astype(bf16), v_var[g, half], preferred_element_type=f32)
                + own_weight.astype(bf16).astype(f32) * dv_all[g][half]
            )
            weighted = part if weighted is None else weighted + part
        total = jnp.where(lane < HEAD_SIZE, totals[0], totals[1])
        rows = (weighted / total).astype(bf16)
        for result_ref in out_refs:
            result_ref[BLOCK:, pair * LANES : (pair + 1) * LANES] = rows
    for shift, result_ref in enumerate(out_refs):
        result_ref[:BLOCK, :] = out_ref[lax.rem(place + shift, n_blocks)]


def out_kernel(place_ref, core_ref, *refs):
    n = len(refs) - 9
    attn_refs, w_refs = refs[:n], refs[n : n + 4]
    res_ref, dres_ref, out_ref, dec_ref, attn_ref = refs[n + 4 :]
    place, core = place_ref[0], core_ref[0]
    width = attn_refs[0].shape[1]
    for shift in range(n):
        attn_ref[lax.rem(place + n - shift, n)] = attn_refs[shift][...]

    def times(rows, w_ref):
        total = None
        for h in range(n):
            weight = w_ref[h * width : (h + 1) * width, :]
            part = jnp.dot(attn_ref[h, rows], weight, preferred_element_type=f32)
            total = part if total is None else total + part
        return total

    blocks = (place, place + n - 1 + 2 * core, place + 1 + 2 * core, place + 2)
    for w_ref, block in zip(w_refs, blocks):
        start = pl.multiple_of(lax.rem(block, n) * width, LANES)
        residual = res_ref[:, pl.ds(start, width)].astype(f32)
        out_ref[:, pl.ds(start, width)] = (residual + times(slice(0, BLOCK), w_ref)).astype(bf16)
    count = dres_ref.shape[1]
    extra = times(slice(BLOCK, BLOCK + DECODE_ROWS), w_refs[0])
    dec_ref[0] = (dres_ref[0].astype(f32) + extra[:count]).astype(bf16)


def shards(
    prefill_residual,
    prompt_queries,
    prompt_keys,
    prompt_values,
    out_weight,
    prompt_token_counts,
    page_dest,
    decode_residual,
    decoded_queries,
    decoded_keys,
    decoded_values,
):
    n_ctx = lax.axis_size("ctx")
    n_req = lax.axis_size("req")
    rows, width = prompt_queries.shape
    q_cols = width // n_ctx
    kv_cols = prompt_keys.shape[1] // n_ctx
    core = lax.axis_index("req") % 2
    vmem = pl.BlockSpec(memory_space=pltpu.VMEM)
    smem = pl.BlockSpec(memory_space=pltpu.SMEM)
    near = lambda a: pltpu.with_memory_space_constraint(a, pltpu.VMEM)

    kv_parts = pl.pallas_call(
        pair_kernel,
        out_shape=jax.ShapeDtypeStruct((n_ctx, rows, 2 * kv_cols), bf16),
        in_specs=[vmem, vmem],
        out_specs=vmem,
        name="pair",
    )(prompt_keys, prompt_values)
    kv = lax.all_to_all(kv_parts, "ctx", 0, 0, tiled=True)
    kv_parts, q_source, w_source = lax.optimization_barrier((kv_parts, prompt_queries, out_weight))
    place = lax.axis_index("ctx").reshape(1)
    send = lambda a, shift: lax.ppermute(a, "ctx", [(i, (i + shift) % n_ctx) for i in range(n_ctx)])
    spread = lambda parts: [parts[0]] + [send(parts[i], i) for i in range(1, n_ctx)]
    q_parts = pl.pallas_call(
        split_kernel,
        out_shape=[jax.ShapeDtypeStruct((rows, q_cols), bf16)] * n_ctx,
        in_specs=[smem, vmem],
        out_specs=[vmem] * n_ctx,
        name="split",
    )(place, q_source)

    place_of = lambda r, c: r * n_ctx + c % n_ctx
    ring = [
        (place_of(r, c), place_of(r, c + (1 if r % 2 == 0 else -1)))
        for r in range(n_req)
        for c in range(n_ctx)
    ]
    swap = [(r, r ^ 1) for r in range(n_req)]

    pages = page_dest.shape[1]
    dest = page_dest[0, :, 0]
    index = jnp.arange(pages, dtype=jnp.int32)
    lane = jnp.sum(
        ((dest[:, None] == dest[None, :]) & (index[None, :] < index[:, None])).astype(jnp.int32), axis=1
    )
    lane_cap = max(2, 2 * pages // n_req)
    slots, q_parts = lax.optimization_barrier(((n_req - 1 - dest) * lane_cap + lane, q_parts))
    order = [list(range(n_req - 1, -1, -1))]
    outgoing = pl.pallas_call(
        page_kernel,
        out_shape=jax.ShapeDtypeStruct((n_req * lane_cap, 2 * PAGE_TOKENS, kv_cols), bf16),
        in_specs=[smem, vmem],
        out_specs=vmem,
        name="pages",
    )(slots, near(kv))
    store = lax.all_to_all(outgoing, "req", 0, 0, axis_index_groups=order, tiled=True)
    store = jnp.flip(store.reshape(n_req, lane_cap, PAGE_TOKENS, 2, kv_cols), 0)
    w_beside = lax.ppermute(w_source, ("req", "ctx"), ring)
    outgoing, w_beside = lax.optimization_barrier((outgoing, w_beside))
    w_beside, q_parts = lax.optimization_barrier((w_beside, q_parts))
    q = spread(q_parts)
    target_page_store = store.reshape(1, n_req * lane_cap, PAGE_TOKENS, 2, kv_cols)

    w_across = lax.ppermute(w_beside, "req", swap)
    w_beyond = lax.ppermute(w_beside, ("req", "ctx"), ring)

    attention = pl.pallas_call(
        attention_kernel,
        out_shape=[jax.ShapeDtypeStruct((rows + DECODE_ROWS, q_cols), bf16)] * n_ctx,
        in_specs=[smem, smem] + [vmem] * (n_ctx + 4),
        out_specs=[vmem] * n_ctx,
        scratch_shapes=[pltpu.VMEM((n_ctx, rows, q_cols), bf16)] * 2
        + [pltpu.VMEM((2, 2, n_ctx * rows, LANES), bf16)] * 2
        + [pltpu.VMEM((DECODE_ROWS, q_cols), f32)]
        + [pltpu.VMEM((DECODE_ROWS, kv_cols), f32)] * 2,
        name="attend",
        cost_estimate=pl.CostEstimate(flops=30000000000, transcendentals=0, bytes_accessed=0),
    )(place, prompt_token_counts, q[0], *map(near, q[1:]), near(kv), decoded_queries, decoded_keys, decoded_values)
    back = spread(attention)
    prefill_out, decode_out = pl.pallas_call(
        out_kernel,
        out_shape=(
            jax.ShapeDtypeStruct(prefill_residual.shape, bf16),
            jax.ShapeDtypeStruct(decode_residual.shape, bf16),
        ),
        in_specs=[smem, smem] + [vmem] * (n_ctx + 6),
        out_specs=(vmem, vmem),
        scratch_shapes=[
            pltpu.VMEM((n_ctx, rows + DECODE_ROWS, q_cols), bf16),
        ],
        name="project",
    )(
        place,
        core.reshape(1),
        back[0],
        *map(near, back[1:]),
        out_weight,
        w_beside,
        w_across,
        w_beyond,
        prefill_residual,
        decode_residual,
    )
    return (prefill_out, target_page_store, decode_out)


def solution(mesh):
    in_specs = (
        P(("req", "ctx"), None),
        P(("req", "ctx"), None),
        P(("req", "ctx"), None),
        P(("req", "ctx"), None),
        P(None, "ctx"),
        P("req", None),
        P("req", None, None),
        P("req", None, "ctx"),
        P("req", None, "ctx"),
        P("req", None, "ctx"),
        P("req", None, "ctx"),
    )
    out_specs = (P(("req", "ctx"), None), P("req", None, None, None, "ctx"), P("req", None, "ctx"))
    return jax.shard_map(shards, mesh=mesh, in_specs=in_specs, out_specs=out_specs, check_vma=False)
```
